512 devices in a mesh: wide: 64 (over y, z), narrow: 8 (over x, core).
Axes of the slice: x: 4, y: 4, z: 16, core: 2. Of those that a mesh axis runs over, the one named last changes fastest.
Arguments:
- integrals: bfloat16 [512, 6, 256, 1024], P(('wide', 'narrow')), may hold values from -1 to 1
- amplitudes: bfloat16 [512, 6, 256, 512], P(('wide', 'narrow')), may hold values from -6 to 6
- tile_count: int32 [512], P(('wide', 'narrow')), may hold values from 1 to 6, as said below
- row_orbitals: int32 [1024, 2], P(('wide', 'narrow')), may hold values from 0 to 575
- virtual_energy: float32 [576], replicated, may hold values from 0.2 to 3
- occupied_energy: float32 [512], replicated, may hold values from -3 to -0.8
- other_terms: float32 [1024, 512], P(('wide', 'narrow')), may hold values from -20 to 20
Outputs:
- update: float32 [1024, 512], P(('wide', 'narrow'))
- update_norm: float32 [], replicated
The draws below stay inside these ranges and needn't reach their ends.
Inputs may be any that keep to these rules, and one draw needn't show every extreme that they name: A device's screened tiles are its first tile_count slots; some device holds 6 in every draw.
All inputs are finite; a program needn't handle non-finite values.
Results may differ from the reference program's by a relative error of at most 0.0003.
Values sent between devices are 32-bit elements; how exact they have to be, the bound alone decides.
A program may use at most 64 MiB of HBM per device.

```python
import math
import jax
import jax.numpy as jnp
from jax import lax

NV = 576
NO = 512
TILE = 256
ROWS = 1024
S_DEV = 6
DEVICES = 512


def draw_tile_count(key, part):
    key_base = jax.random.fold_in(key, 11)
    key_heavy = jax.random.fold_in(key, 12)
    key_peak = jax.random.fold_in(key, 13)
    base_count = jax.random.randint(key_base, (DEVICES,), 1, 3)
    heavy_mask = jax.random.randint(key_heavy, (DEVICES,), 0, 8) == 0
    peak_device = jax.random.randint(key_peak, (), 0, DEVICES)
    device_ids = jnp.arange(DEVICES, dtype=jnp.int32)
    return jnp.where(heavy_mask | (device_ids == peak_device), S_DEV, base_count).astype(jnp.int32)


def draw_integrals(key, part):
    key_noise = jax.random.fold_in(key, 21)
    key_pair = jax.random.fold_in(key, 22)
    key_mean = jax.random.fold_in(key, 23)
    weight_scale = (2.0 * TILE * DEVICES) ** (-0.5)
    mean_scale = (1.0 * TILE * DEVICES) ** (-0.5)
    pairing = jax.random.permutation(key_pair, DEVICES).astype(jnp.int32)
    row_block = (jnp.arange(ROWS, dtype=jnp.int32) // (ROWS // DEVICES)).astype(jnp.int32)
    spike = jnp.where(pairing[:, None] == row_block[None, :], 6.0, 1.0).astype(jnp.float32)
    noise = jnp.clip(jax.random.normal(key_noise, (DEVICES, S_DEV, TILE, ROWS), jnp.float32), -4.0, 4.0)
    row_mean = jax.random.uniform(key_mean, (ROWS,), jnp.float32, -1.5, 1.5)
    value = weight_scale * (noise * spike[:, None, None, :] + mean_scale * row_mean[None, None, None, :])
    return value.astype(jnp.bfloat16)


def draw_amplitudes(key, part):
    key_noise = jax.random.fold_in(key, 31)
    key_column = jax.random.fold_in(key, 32)
    noise = jnp.clip(jax.random.normal(key_noise, (DEVICES, S_DEV, TILE, NO), jnp.float32), -4.5, 4.5)
    column_offset = jax.random.uniform(key_column, (NO,), jnp.float32, -1.0, 1.0)
    return (noise + column_offset[None, None, None, :]).astype(jnp.bfloat16)


def draw_other_terms(key, part):
    row_place = (jnp.arange(ROWS, dtype=jnp.float32) / ROWS)[:, None]
    col_place = (jnp.arange(NO, dtype=jnp.float32) / NO)[None, :]
    noise = jnp.clip(jax.random.normal(key, (ROWS, NO), jnp.float32), -6.0, 6.0)
    scale = 0.3 * jnp.power(10.0, 0.5 * row_place + 0.5 * col_place)
    return (noise * scale).astype(jnp.float32)


def with_ends(entries, stream_key, low, high):
    extent = entries.shape
    spot = [jax.random.randint(jax.random.fold_in(stream_key, axis), (), 0, extent[axis]) for axis in range(len(extent))]
    entries = entries.at[tuple(spot)].set(low)
    longest = extent.index(max(extent))
    spot[longest] = (spot[longest] + 1) % extent[longest]
    return entries.at[tuple(spot)].set(high)


def setup_inputs(seed: int = 0) -> dict:
    splits = jax.random.split(jax.random.key(seed), 8)
    return {
        "integrals": draw_integrals(jax.random.fold_in(splits[7], 71), 0),
        "amplitudes": draw_amplitudes(jax.random.fold_in(splits[7], 71), 0),
        "tile_count": draw_tile_count(jax.random.fold_in(splits[7], 71), 0),
        "row_orbitals": with_ends(jax.random.randint(splits[3], (ROWS, 2), 0, NV), jax.random.fold_in(splits[3], 1), 0, NV - 1).astype(jnp.int32),
        "virtual_energy": jnp.clip(jnp.exp(jax.random.uniform(splits[4], (NV,), jnp.float32, math.log(0.2), math.log(3.0))), 0.2, 3.0),
        "occupied_energy": jnp.clip(jax.random.uniform(splits[5], (NO,), jnp.float32, -3.0, -0.8), -3.0, -0.8),
        "other_terms": draw_other_terms(jax.random.fold_in(splits[7], 71), 0),
    }


def reference(integrals, amplitudes, tile_count, row_orbitals, virtual_energy, occupied_energy, other_terms):

    def device_step(running, items):
        tile_block, amp_rows, live_count = items

        def add_tile(slot_index, partial_value):
            tile_one = lax.dynamic_index_in_dim(tile_block, slot_index, 0, keepdims=False)
            amp_one = lax.dynamic_index_in_dim(amp_rows, slot_index, 0, keepdims=False)
            return partial_value + lax.dot_general(tile_one, amp_one, (((0,), (0,)), ((), ())), preferred_element_type=jnp.float32)
        return (lax.fori_loop(jnp.int32(0), live_count, add_tile, running), None)
    ladder, _ = lax.scan(device_step, jnp.zeros((ROWS, NO), jnp.float32), (integrals, amplitudes, tile_count))
    first_energy = virtual_energy[row_orbitals[:, 0]]
    second_energy = virtual_energy[row_orbitals[:, 1]]
    denominator = occupied_energy[None, :] - (first_energy + second_energy)[:, None]
    update = (ladder + other_terms) / denominator
    update_norm = jnp.sqrt(jnp.sum(update * update) / (ROWS * NO))
    return (update, update_norm)
```

```python
import functools

import jax
import jax.numpy as jnp
from jax import lax
from jax.experimental import pallas as pl
from jax.experimental.pallas import tpu as pltpu
from jax.sharding import PartitionSpec as P

MESH = pl.DeviceIdType.MESH
NX, NY, NZ = 4, 4, 16
SLOTS, TILE = 6, 256
HOPS = (2, 1, 3)
Z_HOPS = (8, 7, 9, 6, 10, 5, 11, 4, 12, 3, 13, 2, 14, 1, 15)


def wait_bytes(ref, sem):
    pltpu.make_async_copy(ref, ref, sem).wait()


def kernel(
    integrals, amplitudes, count, orbitals, virtual, occupied, other,
    out, norm,
    amp, tiles, mine, theirs, core_in,
    x_in, y_in, y_sum, y2_in, x_sum, x2_in, final, z_in,
    early_out, early_in, late_out, late_in, za, zb,
    amp_sem, tile_sem, core_send, core_recv, x_send, x_recv, y_send, y_recv,
    y2_send, y2_recv, x2_send, x2_recv, z_send, z_recv,
    early_send, early_recv, late_send, late_recv, za_send, za_recv, zb_send, zb_recv,
):
    wide, narrow = lax.axis_index("wide"), lax.axis_index("narrow")
    y, z = wide // NZ, wide % NZ
    x, c = narrow // 2, narrow % 2

    def at(x=x, y=y, z=z, c=c):
        return (y * NZ + z, x * 2 + c)

    def send(src, dst, send_sem, recv_sem, device):
        pltpu.make_async_remote_copy(
            src_ref=src, dst_ref=dst, send_sem=send_sem, recv_sem=recv_sem,
            device_id=device, device_id_type=MESH,
        ).start()

    rank = (y * NX + x) * 2 + c
    order = [(y + hop) % NY for hop in HOPS] + [y]

    for half, cc in enumerate((1 - c, c)):
        pltpu.make_async_copy(
            amplitudes.at[0, :, :, pl.ds(pl.multiple_of(cc * 256, 256), 256)],
            amp.at[half], amp_sem.at[half],
        ).start()
    for k in range(4):
        pltpu.make_async_copy(
            integrals.at[0, :, :, pl.ds(pl.multiple_of(order[k] * 256, 256), 256)],
            tiles.at[k], tile_sem.at[k],
        ).start()

    barrier = pltpu.get_barrier_semaphore()

    def greet(device):
        pl.semaphore_signal(barrier, inc=1, device_id=device, device_id_type=MESH)

    for hop in range(1, NZ):
        greet(at(z=(z + hop) % NZ))
    for hop in range(1, 2 * NX * NY):
        r = (rank + hop) % (2 * NX * NY)
        greet(at(x=(r // 2) % NX, y=r // (2 * NX), c=r % 2))

    pair = x + 1 - 2 * (x % 2)
    place = 2 * (x % 2) + c
    column = 2 * c + x % 2
    partners = ((pair, 1 - c), (pair, c), (x, 1 - c))
    for i in range(2):
        level = virtual[orbitals[i, 0]] + virtual[orbitals[i, 1]]
        denominator = occupied[...] - level
        for t in range(4):
            early_out[t, i : i + 1, :] = other[i : i + 1, t * 128 : (t + 1) * 128]
            early_out[t, 2 + i : 3 + i, :] = denominator[:, t * 128 : (t + 1) * 128]

    live = count[0]
    for half in range(2):
        wait_bytes(amp.at[half], amp_sem.at[half])
        for s in range(SLOTS):
            keep = jnp.full((TILE, 256), live, jnp.int32) > s
            value = amp[half, s]
            amp[half, s] = jnp.where(keep, value, jnp.zeros_like(value))

    def multiply(k, half, dst):
        product = lax.dot_general(
            tiles[k].reshape(SLOTS * TILE, 256), amp[half].reshape(SLOTS * TILE, 256),
            (((0,), (0,)), ((), ())), preferred_element_type=jnp.float32,
        ).reshape(NZ, 2, 8, 256)
        for xx in range(NX):
            dst[k, xx] = product[:, xx // 2, :, (xx % 2) * 128 : (xx % 2 + 1) * 128]

    def core_done(k):
        wait_bytes(core_in.at[k], core_recv.at[k])
        mine[k] = mine[k] + core_in[k]
        for n, hop in enumerate(HOPS):
            xt = (x + hop) % NX
            send(mine.at[k, xt, pl.ds(0, 8)], x_in.at[k, n], x_send, x_recv.at[k], at(x=xt))
        if k < 3:
            send(mine.at[k, :, pl.ds(8, 8)], y_in.at[k], y_send, y_recv.at[k], at(y=order[k]))

    for k in range(4):
        wait_bytes(tiles.at[k], tile_sem.at[k])
        multiply(k, 0, theirs)
        if k == 0:
            pl.semaphore_wait(barrier, (NZ - 1) + (2 * NX * NY - 1))
            for xp, cp in partners:
                send(early_out.at[2 * cp + xp % 2], early_in.at[place], early_send, early_recv, at(x=xp, c=cp))
            early_in[place] = early_out[column]
        send(theirs.at[k], core_in.at[k], core_send, core_recv.at[k], at(c=1 - c))
        multiply(k, 1, mine)
        if k > 0:
            core_done(k - 1)
    core_done(3)

    for k in range(4):
        wait_bytes(x_in.at[k], x_recv.at[k])
        total = mine[k, x, 0:8] + x_in[k, 0] + x_in[k, 1] + x_in[k, 2]
        if k < 3:
            y_sum[k] = total
            send(y_sum.at[k], y2_in.at[k], y2_send, y2_recv, at(y=order[k]))
        else:
            final[0:8] = total
    for k in range(3):
        wait_bytes(y_in.at[k], y_recv.at[k])
    x_sum[...] = mine[3, :, 8:16] + y_in[0] + y_in[1] + y_in[2]
    for n, hop in enumerate(HOPS):
        xt = (x + hop) % NX
        send(x_sum.at[xt], x2_in.at[n], x2_send, x2_recv, at(x=xt))
    wait_bytes(y2_in, y2_recv)
    final[0:8] = final[0:8] + y2_in[0] + y2_in[1] + y2_in[2]
    wait_bytes(x2_in, x2_recv)
    final[8:16] = x_sum[x] + x2_in[0] + x2_in[1] + x2_in[2]

    for n, hop in enumerate(Z_HOPS):
        zt = (z + hop) % NZ
        send(final.at[zt], z_in.at[n], z_send, z_recv, at(z=zt))
    wait_bytes(early_in.at[pl.ds(0, 3)], early_recv)
    wait_bytes(z_in, z_recv)
    ladder = final[z] + jnp.sum(z_in[...], axis=0)
    other_tile = jnp.concatenate([early_in[g, 0:2] for g in range(4)], axis=0)
    denominator_tile = jnp.concatenate([early_in[g, 2:4] for g in range(4)], axis=0)
    update = (ladder + other_tile) / denominator_tile

    za[z] = jnp.sum(update * update, axis=0, keepdims=True)
    for n, hop in enumerate(Z_HOPS):
        zt = (z + hop) % NZ
        send(za.at[z], za.at[z], za_send, za_recv, at(z=zt))
    for g in range(4):
        late_out[g] = update[2 * g : 2 * g + 2]
    for xp, cp in partners:
        send(late_out.at[2 * (xp % 2) + cp], late_in.at[column], late_send, late_recv, at(x=xp, c=cp))
    late_in[column] = late_out[place]
    wait_bytes(za.at[pl.ds(0, NZ - 1)], za_recv)
    zb[rank] = jnp.sum(za[...], axis=0)
    for hop in range(1, 2 * NX * NY):
        r = (rank + hop) % (2 * NX * NY)
        send(zb.at[rank], zb.at[rank], zb_send, zb_recv, at(x=(r // 2) % NX, y=r // (2 * NX), c=r % 2))
    wait_bytes(late_in.at[pl.ds(0, 3)], late_recv)
    for t in range(4):
        out[:, t * 128 : (t + 1) * 128] = late_in[t]
    wait_bytes(zb.at[pl.ds(0, 2 * NX * NY - 1)], zb_recv)
    squares = jnp.sum(jnp.sum(zb[...], axis=0), axis=1, keepdims=True)
    norm[...] = jnp.sqrt(squares / (NX * NY * NZ * 2 * 2 * 512))

    wait_bytes(core_in, core_send)
    wait_bytes(x_in, x_send)
    wait_bytes(y_in, y_send)
    wait_bytes(y2_in, y2_send)
    wait_bytes(x2_in, x2_send)
    wait_bytes(z_in, z_send)
    wait_bytes(early_in.at[pl.ds(0, 3)], early_send)
    wait_bytes(late_in.at[pl.ds(0, 3)], late_send)
    wait_bytes(za.at[pl.ds(0, NZ - 1)], za_send)
    wait_bytes(zb.at[pl.ds(0, 2 * NX * NY - 1)], zb_send)


def shards(
    integrals, amplitudes, tile_count, row_orbitals, virtual_energy, occupied_energy, other_terms
):
    f32 = jnp.float32
    vmem = pl.BlockSpec(memory_space=pltpu.VMEM)
    smem = pl.BlockSpec(memory_space=pltpu.SMEM)
    hbm = pl.BlockSpec(memory_space=pl.ANY)
    dma = pltpu.SemaphoreType.DMA
    update, norm = pl.pallas_call(
        kernel,
        out_shape=(
            jax.ShapeDtypeStruct(other_terms.shape, f32),
            jax.ShapeDtypeStruct((1, 1), f32),
        ),
        in_specs=[hbm, hbm, smem, smem, smem, vmem, vmem],
        out_specs=(vmem, vmem),
        scratch_shapes=[
            pltpu.VMEM((2, SLOTS, TILE, 256), jnp.bfloat16),
            pltpu.VMEM((4, SLOTS, TILE, 256), jnp.bfloat16),
            pltpu.VMEM((4, NX, NZ, 8, 128), f32),
            pltpu.VMEM((4, NX, NZ, 8, 128), f32),
            pltpu.VMEM((4, NX, NZ, 8, 128), f32),
            pltpu.VMEM((4, 3, 8, 8, 128), f32),
            pltpu.VMEM((3, NX, 8, 8, 128), f32),
            pltpu.VMEM((3, 8, 8, 128), f32),
            pltpu.VMEM((3, 8, 8, 128), f32),
            pltpu.VMEM((NX, 8, 8, 128), f32),
            pltpu.VMEM((3, 8, 8, 128), f32),
            pltpu.VMEM((NZ, 8, 128), f32),
            pltpu.VMEM((NZ - 1, 8, 128), f32),
            pltpu.VMEM((4, 4, 128), f32),
            pltpu.VMEM((4, 4, 128), f32),
            pltpu.VMEM((4, 2, 128), f32),
            pltpu.VMEM((4, 2, 128), f32),
            pltpu.VMEM((NZ, 1, 128), f32),
            pltpu.VMEM((2 * NX * NY, 1, 128), f32),
            dma((2,)), dma((4,)), dma, dma((4,)), dma, dma((4,)), dma, dma((3,)),
            dma, dma, dma, dma, dma, dma,
            dma, dma, dma, dma, dma, dma, dma, dma,
        ],
        compiler_params=pltpu.CompilerParams(
            collective_id=0, has_side_effects=True, vmem_limit_bytes=32 << 20
        ),
    )(
        integrals, amplitudes, tile_count, row_orbitals, virtual_energy,
        occupied_energy[None, :], other_terms,
    )
    return (update, norm[0, 0])


def solution(mesh):
    in_specs = (
        P(("wide", "narrow"), None, None, None),
        P(("wide", "narrow"), None, None, None),
        P(("wide", "narrow")),
        P(("wide", "narrow"), None),
        P(),
        P(),
        P(("wide", "narrow"), None),
    )
    out_specs = (P(("wide", "narrow"), None), P())
    return jax.shard_map(shards, mesh=mesh, in_specs=in_specs, out_specs=out_specs, check_vma=False)
```
